768 devices in a mesh: dp: 8 (over x, core), row: 32 (over y, z_hi), col: 3 (over z_lo).
Axes of the slice: x: 4, y: 8, z: 12 (z_hi: 4, z_lo: 3; z = z_hi * 3 + z_lo), core: 2. Of those that a mesh axis runs over, the one named last changes fastest.
Arguments:
- grad_parts: bfloat16 [8, 1, 4096, 3, 4096], P('dp', None, 'row', 'col'), may hold values from -128 to 128
- weights: bfloat16 [1, 4096, 3, 4096], P(None, 'row', 'col', 'dp'), may hold values from -0.09375 to 0.09375
- row_old: float32 [1, 4096], P(None, 'row'), may hold values from 0.5 to 2
- col_old: float32 [1, 3, 4096], P(None, 'col', 'dp'), may hold values from 0.5 to 32
- step_rates: float32 [1], replicated, may hold values from 0.1 to 0.3
Outputs:
- new_weights: bfloat16 [1, 4096, 3, 4096], P(None, 'row', 'col', 'dp')
- row_moment: float32 [1, 4096], P(None, 'row')
- col_moment: float32 [1, 3, 4096], P(None, 'col', 'dp')
The draws below stay inside these ranges and needn't reach their ends.
All inputs are finite; a program needn't handle non-finite values.
Results may differ from the reference program's by a relative error of at most 0.001.
Values sent between devices are 32-bit elements; how exact they have to be, the bound alone decides.
A program may use at most 32 MiB of HBM per device.

```python
import math
import jax
import jax.numpy as jnp
from jax import lax

D = 4096
LAYERS = 1
QKV = 12288
COLS_PART = 4096
N_DP = 8
N_COL = 3


def block_levels(key):
    layer_keys = jax.random.split(key, LAYERS)
    orders = jax.vmap(lambda single: jax.random.permutation(single, N_COL))(layer_keys)
    level = orders.astype(jnp.float32) / max(N_COL - 1, 1)
    return 0.35 * jnp.exp(level * math.log(8.0))


def draw_grad_parts(key, part):
    keys = jax.random.split(key, 5)
    reach = 0.5 * math.log(10.0)
    row_scale = jnp.exp(jax.random.uniform(keys[0], (1, LAYERS, D, N_COL, 1), jnp.float32) * reach)
    col_scale = jnp.exp(jax.random.uniform(keys[1], (1, LAYERS, 1, N_COL, COLS_PART), jnp.float32) * reach)
    amplitude = block_levels(keys[4]).reshape(1, LAYERS, 1, N_COL, 1)
    noise = jnp.clip(jax.random.normal(keys[2], (N_DP, LAYERS, D, N_COL, COLS_PART), jnp.float32), -6.0, 6.0)
    values = jnp.clip(noise * row_scale * col_scale * amplitude / math.sqrt(N_DP), -128.0, 128.0)
    return values.astype(jnp.bfloat16)


def draw_col_old(key, part):
    rise = math.log(16.0)
    place = jnp.arange(COLS_PART, dtype=jnp.float32) / COLS_PART
    ramp = 0.5 * jnp.exp(rise * place)
    factor = jax.random.uniform(key, (LAYERS, N_COL, COLS_PART), jnp.float32, 1.0, 2.0)
    return ramp[None, None, :] * factor


def block_scale(rng, shape, pieces, smallest, top_value):
    factor_of = 1.0
    for axis_at, blocks in pieces:
        draws = jax.random.uniform(jax.random.fold_in(jax.random.fold_in(rng, 6), axis_at), (blocks,), jnp.float32, smallest / len(pieces), top_value / len(pieces))
        factor_of = factor_of * jnp.repeat(jnp.exp(draws), shape[axis_at] // blocks).reshape((-1,) + (1,) * (len(shape) - 1 - axis_at))
    return factor_of


def scatter_about(own_key, extent, scale, bound, cuts=(), kind=jnp.bfloat16):
    entries = scale * jax.random.normal(own_key, extent, jnp.float32)
    if cuts:
        entries = entries * block_scale(own_key, extent, cuts, -0.22, 0.18)
    return jnp.clip(entries, -bound, bound).astype(kind)


def setup_inputs(seed: int = 0) -> dict:
    key_of = jax.random.split(jax.random.key(seed), 6)
    grad_parts = draw_grad_parts(jax.random.fold_in(key_of[5], 71), 0)
    weights = scatter_about(key_of[1], (LAYERS, D, N_COL, COLS_PART), D ** -0.5, 0.09375, ((1, 32), (2, 3), (3, 8)))
    row_old = jnp.clip(jnp.exp(math.log(2.0) - 1.3862944 * jax.random.uniform(key_of[2], (LAYERS, D), jnp.float32) ** block_scale(key_of[2], (LAYERS, D), ((1, 32),), -0.2, 0.2)), 0.5, 2.0)
    col_old = draw_col_old(jax.random.fold_in(key_of[5], 71), 0)
    step_rates = jnp.clip(jnp.exp(jax.random.uniform(key_of[4], (LAYERS,), jnp.float32, math.log(0.1), math.log(0.3))), 0.1, 0.3)
    return dict(grad_parts=grad_parts, weights=weights, row_old=row_old, col_old=col_old, step_rates=step_rates)


def reference(grad_parts, weights, row_old, col_old, step_rates):
    gradient = jnp.zeros(grad_parts.shape[1:], jnp.float32)
    for index in range(N_DP):
        gradient = gradient + grad_parts[index].astype(jnp.float32)
    squares = gradient * gradient + 1e-30
    row_moment = 0.8 * row_old + 0.2 * lax.optimization_barrier(jnp.sum(squares, axis=(2, 3))) / QKV
    col_moment = 0.8 * col_old + 0.2 * lax.optimization_barrier(jnp.sum(squares, axis=1)) / D
    second = row_moment[:, :, None, None] * col_moment[:, None, :, :]
    update = gradient / jnp.sqrt(second)
    update_total = lax.optimization_barrier(jnp.sum(update * update, axis=(1, 2, 3)))
    clip_factor = 1.0 / jnp.maximum(1.0, jnp.sqrt(update_total / (D * QKV)) / 0.2)
    step_size = (step_rates * clip_factor)[:, None, None, None]
    new_weights = (weights.astype(jnp.float32) - step_size * update).astype(jnp.bfloat16)
    return (new_weights, row_moment, col_moment)
```

```python
import functools

import jax
import jax.numpy as jnp
from jax import lax
from jax.experimental import pallas as pl
from jax.experimental.pallas import tpu as pltpu
from jax.sharding import PartitionSpec as P

D = 4096
QKV = 12288
EPS = 1e-30
MESH = pl.DeviceIdType.MESH
CHUNKS = 4


def kernel(n_dp, n_row, n_col, g_hbm, w_ref, ro_ref, co_ref, sr_ref, ow_ref, orow_ref, ocol_ref,
           gb, snd, prt, b1, q1, b2, q2, gf, rowbuf, colbuf, totbuf, cold,
           load_sem, core_send, core_recv, s1_send, s1_recv, s2_send, s2_recv, ar_send, ar_recv):
    rows = gb.shape[0]
    cols = gf.shape[1]
    half = cols // 2
    lanes = 128
    groups = cols // lanes
    rc = rows // CHUNKS
    nx = n_dp // 2
    n_flat = n_dp * n_col

    dp = lax.axis_index("dp")
    row = lax.axis_index("row")
    col = lax.axis_index("col")
    x = lax.div(dp, 2)
    core = lax.rem(dp, 2)
    me = dp * n_col + col
    partner = dp + 1 - 2 * core

    def dev(d, r, c):
        return {"dp": d, "row": r, "col": c}

    def load(k):
        rs = pl.ds(k * rc, rc)
        return pltpu.make_async_copy(g_hbm.at[rs], gb.at[rs], load_sem.at[k])

    for k in range(CHUNKS):
        load(k).start()

    flat_peers = []
    for dc in range(n_col):
        for dd in range(n_dp):
            if dc or dd:
                flat_peers.append((lax.rem(dp + dd, n_dp), lax.rem(col + dc, n_col)))
    row_peers = [lax.rem(row + r, n_row) for r in range(1, n_row)]

    barrier = pltpu.get_barrier_semaphore()
    for d, c in flat_peers:
        pl.semaphore_signal(barrier, inc=1, device_id=dev(d, row, c), device_id_type=MESH)
    for r in row_peers:
        pl.semaphore_signal(barrier, inc=1, device_id=dev(dp, r, col), device_id_type=MESH)

    def block(k, rel, who):
        j = 2 * lax.rem(x + rel, nx) + who
        start = pl.multiple_of(j * cols, cols)
        return gb[pl.ds(k * rc, rc), pl.ds(start, cols)].astype(jnp.float32)

    def core_copy(k):
        return pltpu.make_async_remote_copy(
            src_ref=snd.at[k], dst_ref=prt.at[k], send_sem=core_send.at[k], recv_sem=core_recv.at[k],
            device_id=dev(partner, row, col), device_id_type=MESH)

    right = 2 * lax.rem(x + 1, nx) + core
    left = 2 * lax.rem(x + nx - 1, nx) + core

    def hop(buf, out, k, side, send_sem, recv_sem):
        return pltpu.make_async_remote_copy(
            src_ref=buf.at[k, side], dst_ref=out.at[k, side], send_sem=send_sem.at[k, side],
            recv_sem=recv_sem.at[k, side],
            device_id=dev(right if side == 0 else left, row, col), device_id_type=MESH)

    for k in range(CHUNKS):
        load(k).wait()
        for rel in range(nx):
            snd[k, rel] = block(k, rel, 1 - core)
        if k == 0:
            pl.semaphore_wait(barrier, len(flat_peers) + len(row_peers))
        core_copy(k).start()

    def stage1(k):
        core_copy(k).wait_recv()
        far = block(k, 2, core) + prt[k, 2]
        b1[k, 0] = far[:, :half]
        b1[k, 1] = far[:, half:]
        for side in range(2):
            hop(b1, q1, k, side, s1_send, s1_recv).start()

    def stage2(k):
        for side, rel in ((0, 1), (1, nx - 1)):
            hop(b1, q1, k, side, s1_send, s1_recv).wait_recv()
            near = block(k, rel, core) + prt[k, rel]
            lo, hi = near[:, :half], near[:, half:]
            if side == 0:
                lo = lo + q1[k, 0]
            else:
                hi = hi + q1[k, 1]
            b2[k, side, :, :half] = lo
            b2[k, side, :, half:] = hi
            hop(b2, q2, k, side, s2_send, s2_recv).start()

    def finish(k):
        own = block(k, 0, core) + prt[k, 0]
        for side in range(2):
            hop(b2, q2, k, side, s2_send, s2_recv).wait_recv()
            own = own + q2[k, side]
        gf[pl.ds(k * rc, rc), :] = own

    for k in range(CHUNKS + 2):
        if k < CHUNKS:
            stage1(k)
        if 0 <= k - 1 < CHUNKS:
            stage2(k - 1)
        if k - 2 >= 0:
            finish(k - 2)

    def exchange_flat(buf, i):
        for d, c in flat_peers:
            pltpu.make_async_remote_copy(
                src_ref=buf.at[me], dst_ref=buf.at[me], send_sem=ar_send.at[i], recv_sem=ar_recv.at[i],
                device_id=dev(d, row, c), device_id_type=MESH).start()

    def all_of(buf, n, i):
        return pltpu.make_async_remote_copy(
            src_ref=buf.at[pl.ds(0, n)], dst_ref=buf.at[pl.ds(0, n)], send_sem=ar_send.at[i], recv_sem=ar_recv.at[i],
            device_id=dev(partner, row, col), device_id_type=MESH)

    acc = jnp.zeros((rows, lanes), jnp.float32)
    for q in range(groups):
        v = gf[:, q * lanes:(q + 1) * lanes]
        sq = v * v + EPS
        acc = acc + sq
        colbuf[row, q:q + 1, :] = jnp.sum(sq, axis=0, keepdims=True)
        cold[q:q + 1, :] = co_ref[:, q * lanes:(q + 1) * lanes]
    rowbuf[me] = jnp.sum(acc.T, axis=0, keepdims=True)
    exchange_flat(rowbuf, 0)
    all_of(rowbuf, n_flat - 1, 0).wait_recv()
    row_sum = jnp.sum(rowbuf[...], axis=0)
    row_moment = 0.8 * ro_ref[...] + 0.2 * row_sum / QKV
    orow_ref[...] = row_moment
    scale = jnp.broadcast_to(lax.rsqrt(row_moment), (lanes, rows)).T

    for q in range(groups):
        h = gf[:, q * lanes:(q + 1) * lanes] * scale
        gf[:, q * lanes:(q + 1) * lanes] = h
        colbuf[row, groups + q:groups + q + 1, :] = jnp.sum(h * h, axis=0, keepdims=True)
    for r in row_peers:
        pltpu.make_async_remote_copy(
            src_ref=colbuf.at[row], dst_ref=colbuf.at[row], send_sem=ar_send.at[1], recv_sem=ar_recv.at[1],
            device_id=dev(dp, r, col), device_id_type=MESH).start()
    all_of(colbuf, n_row - 1, 1).wait_recv()
    both = jnp.sum(colbuf[...], axis=0)
    col_moment = 0.8 * cold[...] + 0.2 * both[:groups] / D
    part = both[groups:] / col_moment
    totbuf[me] = jnp.sum(part, axis=0, keepdims=True)
    exchange_flat(totbuf, 2)
    inv = lax.rsqrt(col_moment)
    for q in range(groups):
        ocol_ref[:, q * lanes:(q + 1) * lanes] = col_moment[q:q + 1]
        gf[:, q * lanes:(q + 1) * lanes] = gf[:, q * lanes:(q + 1) * lanes] * inv[q:q + 1]
    all_of(totbuf, n_flat - 1, 2).wait_recv()
    total = jnp.sum(jnp.sum(totbuf[...], axis=0), axis=1, keepdims=True)
    clip = 1.0 / jnp.maximum(1.0, jnp.sqrt(total / (D * QKV)) / 0.2)
    step = sr_ref[0] * clip
    ow_ref[...] = (w_ref[...].astype(jnp.float32) - step * gf[...]).astype(jnp.bfloat16)

    for k in range(CHUNKS):
        core_copy(k).wait_send()
        for side in range(2):
            hop(b1, q1, k, side, s1_send, s1_recv).wait_send()
            hop(b2, q2, k, side, s2_send, s2_recv).wait_send()
    all_of(rowbuf, n_flat - 1, 0).wait_send()
    all_of(colbuf, n_row - 1, 1).wait_send()
    all_of(totbuf, n_flat - 1, 2).wait_send()


def solution(mesh):
    n_dp, n_row, n_col = (mesh.shape[a] for a in ("dp", "row", "col"))

    def per_device(grad_parts, weights, row_old, col_old, step_rates):
        rows, width = grad_parts.shape[2], grad_parts.shape[4]
        cols = weights.shape[3]
        nx = n_dp // 2
        rc = rows // CHUNKS
        f32 = jnp.float32
        vmem = pl.BlockSpec(memory_space=pltpu.VMEM)
        dma = pltpu.SemaphoreType.DMA
        new_w, row_moment, col_moment = pl.pallas_call(
            functools.partial(kernel, n_dp, n_row, n_col),
            out_shape=(
                jax.ShapeDtypeStruct((rows, cols), jnp.bfloat16),
                jax.ShapeDtypeStruct((1, rows), f32),
                jax.ShapeDtypeStruct((1, cols), f32),
            ),
            in_specs=[pl.BlockSpec(memory_space=pl.ANY), vmem, vmem, vmem, pl.BlockSpec(memory_space=pltpu.SMEM)],
            out_specs=(vmem, vmem, vmem),
            scratch_shapes=[
                pltpu.VMEM((rows, width), jnp.bfloat16),
                pltpu.VMEM((CHUNKS, nx, rc, cols), f32),
                pltpu.VMEM((CHUNKS, nx, rc, cols), f32),
                pltpu.VMEM((CHUNKS, 2, rc, cols // 2), f32),
                pltpu.VMEM((CHUNKS, 2, rc, cols // 2), f32),
                pltpu.VMEM((CHUNKS, 2, rc, cols), f32),
                pltpu.VMEM((CHUNKS, 2, rc, cols), f32),
                pltpu.VMEM((rows, cols), f32),
                pltpu.VMEM((n_dp * n_col, 1, 128), f32),
                pltpu.VMEM((n_row, 8, 128), f32),
                pltpu.VMEM((n_dp * n_col, 1, 128), f32),
                pltpu.VMEM((4, 128), f32),
                dma((CHUNKS,)),
                dma((CHUNKS,)), dma((CHUNKS,)),
                dma((CHUNKS, 2)), dma((CHUNKS, 2)),
                dma((CHUNKS, 2)), dma((CHUNKS, 2)),
                dma((3,)), dma((3,)),
            ],
            compiler_params=pltpu.CompilerParams(collective_id=0, has_side_effects=True, vmem_limit_bytes=24 << 20),
        )(grad_parts.reshape(rows, width), weights.reshape(rows, cols), row_old, col_old.reshape(1, cols), step_rates)
        return new_w.reshape(weights.shape), row_moment, col_moment.reshape(col_old.shape)

    in_specs = (
        P("dp", None, "row", "col", None),
        P(None, "row", "col", "dp"),
        P(None, "row"),
        P(None, "col", "dp"),
        P(),
    )
    out_specs = (P(None, "row", "col", "dp"), P(None, "row"), P(None, "col", "dp"))
    return jax.shard_map(per_device, mesh=mesh, in_specs=in_specs, out_specs=out_specs, check_vma=False)
```

```python
import functools

import jax
import jax.numpy as jnp
from jax import lax
from jax.experimental import pallas as pl
from jax.experimental.pallas import tpu as pltpu
from jax.sharding import PartitionSpec as P

D = 4096
QKV = 12288
EPS = 1e-30
MESH = pl.DeviceIdType.MESH
CHUNKS = 4
LANES = 128
NX, NCORE, NY, NZHI, NZLO = 4, 2, 8, 4, 3
NZ = NZHI * NZLO


def kernel(g_hbm, w_hbm, ro_hbm, co_hbm, sr_hbm, ow_ref, orow_ref, ocol_ref,
           gb, snd, prt, b1, q1, b2, q2, gf, wv, ro, co, sr, rowbuf, colbuf, totbuf,
           load_sem, misc_sem, core_send, core_recv, s1_send, s1_recv, s2_send, s2_recv, ar_send, ar_recv, met):
    rows, cols = gf.shape
    half = cols // 2
    groups = cols // LANES
    rc = rows // CHUNKS
    n_flat = NX * NCORE * NZLO
    n_row = NY * NZHI

    dp = lax.axis_index("dp")
    row = lax.axis_index("row")
    col = lax.axis_index("col")
    x, core = lax.div(dp, NCORE), lax.rem(dp, NCORE)
    y, zhi = lax.div(row, NZHI), lax.rem(row, NZHI)
    z = zhi * NZLO + col
    me = dp * NZLO + col

    def at(dx=0, dc=0, dy=0, dz=0):
        zz = lax.rem(z + dz + NZ, NZ)
        return {
            "dp": lax.rem(x + dx + NX, NX) * NCORE + lax.rem(core + dc, NCORE),
            "row": lax.rem(y + dy + NY, NY) * NZHI + lax.div(zz, NZLO),
            "col": lax.rem(zz, NZLO),
        }

    def flat_at(dx, dc, k):
        return {"dp": lax.rem(x + dx, NX) * NCORE + lax.rem(core + dc, NCORE), "row": row, "col": lax.rem(col + k, NZLO)}

    def row_at(dy, dz):
        return {"dp": dp, "row": lax.rem(y + dy, NY) * NZHI + lax.rem(zhi + dz, NZHI), "col": col}

    flat_peers = [flat_at(dx, dc, k) for dx in (2, 1, 3, 0) for k in (1, 2, 0) for dc in (1, 0) if dx or dc or k]
    row_peers = [row_at(dy, dz) for dy, dz in sorted(
        ((dy, dz) for dy in range(NY) for dz in range(NZHI) if dy or dz),
        key=lambda p: -(min(p[0], NY - p[0]) + 3 * min(p[1], NZHI - p[1])))]

    near = [at(dc=1), at(dx=1), at(dx=-1), at(dy=1), at(dy=-1), at(dz=1), at(dz=-1)]
    steps = [
        near,
        [at(dc=1), at(dx=2), at(dy=2), at(dy=-2), at(dz=2), at(dz=-2)],
        [at(dc=1), at(dz=3), at(dz=-3)],
        [at(dz=3), at(dz=-3)],
    ]

    barrier = pltpu.get_barrier_semaphore()
    for d in near:
        pl.semaphore_signal(barrier, inc=1, device_id=d, device_id_type=MESH)

    def tell(s):
        for d in steps[s]:
            pl.semaphore_signal(met.at[s], inc=1, device_id=d, device_id_type=MESH)

    def hear(s):
        pl.semaphore_wait(met.at[s], len(steps[s]))

    def load(rel, who):
        j = lax.rem(x + rel, NX) * NCORE + (core if who == 0 else 1 - core)
        i = 2 * rel + who
        return pltpu.make_async_copy(
            g_hbm.at[:, pl.ds(pl.multiple_of(j * cols, cols), cols)], gb.at[i], load_sem.at[i])

    order = (2, 1, 3, 0)
    for rel in order:
        for who in (1, 0):
            load(rel, who).start()
    misc = [pltpu.make_async_copy(a, b, misc_sem.at[i])
            for i, (a, b) in enumerate(((w_hbm, wv), (ro_hbm, ro), (co_hbm, co), (sr_hbm, sr)))]
    for m in misc:
        m.start()

    def part(rel, who, rs):
        return gb[2 * rel + who, rs, :].astype(jnp.float32)

    def chunk(k):
        return pl.ds(k * rc, rc)

    def core_copy(i):
        if i < CHUNKS:
            src, dst = snd.at[2, chunk(i)], prt.at[2, chunk(i)]
        else:
            src, dst = snd.at[order[i - CHUNKS + 1]], prt.at[order[i - CHUNKS + 1]]
        return pltpu.make_async_remote_copy(
            src_ref=src, dst_ref=dst, send_sem=core_send.at[i], recv_sem=core_recv.at[i],
            device_id=at(dc=1), device_id_type=MESH)

    n_core = CHUNKS + 3

    def hop(buf, out, k, side, send_sem, recv_sem):
        return pltpu.make_async_remote_copy(
            src_ref=buf.at[k, side], dst_ref=out.at[k, side], send_sem=send_sem.at[k, side],
            recv_sem=recv_sem.at[k, side],
            device_id=at(dx=1 if side == 0 else -1), device_id_type=MESH)

    whole = pl.ds(0, rows)
    for n, rel in enumerate(order):
        load(rel, 1).wait()
        snd[rel] = part(rel, 1, whole)
        if n == 0:
            pl.semaphore_wait(barrier, len(near))
            for i in range(CHUNKS):
                core_copy(i).start()
        else:
            core_copy(CHUNKS + n - 1).start()
    tell(0)

    load(2, 0).wait()
    for k in range(CHUNKS):
        core_copy(k).wait_recv()
        far = part(2, 0, chunk(k)) + prt[2, chunk(k), :]
        b1[k, 0] = far[:, :half]
        b1[k, 1] = far[:, half:]
        for side in range(2):
            hop(b1, q1, k, side, s1_send, s1_recv).start()
    hear(0)
    tell(1)
    load(1, 0).wait()
    load(3, 0).wait()
    core_copy(CHUNKS).wait_recv()
    core_copy(CHUNKS + 1).wait_recv()
    for k in range(CHUNKS):
        for side, rel in ((0, 1), (1, 3)):
            near_sum = part(rel, 0, chunk(k)) + prt[rel, chunk(k), :]
            lo, hi = near_sum[:, :half], near_sum[:, half:]
            hop(b1, q1, k, side, s1_send, s1_recv).wait_recv()
            if side == 0:
                lo = lo + q1[k, 0]
            else:
                hi = hi + q1[k, 1]
            b2[k, side, :, :half] = lo
            b2[k, side, :, half:] = hi
            hop(b2, q2, k, side, s2_send, s2_recv).start()
    hear(1)
    tell(2)
    load(0, 0).wait()
    core_copy(CHUNKS + 2).wait_recv()
    for m in misc:
        m.wait()
    for k in range(CHUNKS):
        own = part(0, 0, chunk(k)) + prt[0, chunk(k), :]
        for side in range(2):
            hop(b2, q2, k, side, s2_send, s2_recv).wait_recv()
            own = own + q2[k, side]
        gf[chunk(k), :] = own

    def exchange(buf, slot, peers, i):
        for d in peers:
            pltpu.make_async_remote_copy(
                src_ref=buf.at[slot], dst_ref=buf.at[slot], send_sem=ar_send.at[i], recv_sem=ar_recv.at[i],
                device_id=d, device_id_type=MESH).start()

    def all_of(buf, n, i):
        return pltpu.make_async_remote_copy(
            src_ref=buf.at[pl.ds(0, n)], dst_ref=buf.at[pl.ds(0, n)], send_sem=ar_send.at[i], recv_sem=ar_recv.at[i],
            device_id=at(dc=1), device_id_type=MESH)

    def lane(q):
        return slice(q * LANES, (q + 1) * LANES)

    acc = jnp.zeros((rows, LANES), jnp.float32)
    for q in range(groups):
        v = gf[:, lane(q)]
        acc = acc + (v * v + EPS)
    rowbuf[me] = jnp.sum(acc.T, axis=0, keepdims=True)
    hear(2)
    exchange(rowbuf, me, flat_peers, 0)
    tell(3)
    for q in range(groups):
        v = gf[:, lane(q)]
        colbuf[row, q:q + 1, :] = jnp.sum(v * v + EPS, axis=0, keepdims=True)
    all_of(rowbuf, n_flat - 1, 0).wait_recv()
    row_sum = jnp.sum(rowbuf[...], axis=0)
    row_moment = 0.8 * ro[...] + 0.2 * row_sum / QKV
    orow_ref[...] = row_moment
    scale = jnp.broadcast_to(lax.rsqrt(row_moment), (LANES, rows)).T

    for q in range(groups):
        h = gf[:, lane(q)] * scale
        gf[:, lane(q)] = h
        colbuf[row, groups + q:groups + q + 1, :] = jnp.sum(h * h, axis=0, keepdims=True)
    hear(3)
    exchange(colbuf, row, row_peers, 1)
    all_of(colbuf, n_row - 1, 1).wait_recv()
    both = jnp.sum(colbuf[...], axis=0)
    total_part = jnp.zeros((1, LANES), jnp.float32)
    for q in range(groups):
        col_moment = 0.8 * co[:, lane(q)] + 0.2 * both[q:q + 1] / D
        ocol_ref[:, lane(q)] = col_moment
        total_part = total_part + both[groups + q:groups + q + 1] / col_moment
    totbuf[me] = total_part
    exchange(totbuf, me, flat_peers, 2)
    for q in range(groups):
        gf[:, lane(q)] = gf[:, lane(q)] * lax.rsqrt(ocol_ref[:, lane(q)])
    all_of(totbuf, n_flat - 1, 2).wait_recv()
    total = jnp.sum(jnp.sum(totbuf[...], axis=0), axis=1, keepdims=True)
    clip = 1.0 / jnp.maximum(1.0, jnp.sqrt(total / (D * QKV)) / 0.2)
    step = sr[...] * clip
    ow_ref[...] = (wv[...].astype(jnp.float32) - step * gf[...]).astype(jnp.bfloat16)

    for i in range(n_core):
        core_copy(i).wait_send()
    for k in range(CHUNKS):
        for side in range(2):
            hop(b1, q1, k, side, s1_send, s1_recv).wait_send()
            hop(b2, q2, k, side, s2_send, s2_recv).wait_send()
    all_of(rowbuf, n_flat - 1, 0).wait_send()
    all_of(colbuf, n_row - 1, 1).wait_send()
    all_of(totbuf, n_flat - 1, 2).wait_send()


def solution(mesh):
    def per_device(grad_parts, weights, row_old, col_old, step_rates):
        rows, width = grad_parts.shape[2], grad_parts.shape[4]
        cols = weights.shape[3]
        rc = rows // CHUNKS
        f32 = jnp.float32
        vmem = pl.BlockSpec(memory_space=pltpu.VMEM)
        hbm = pl.BlockSpec(memory_space=pltpu.HBM)
        dma = pltpu.SemaphoreType.DMA
        shapes = (
            jax.ShapeDtypeStruct((rows, cols), jnp.bfloat16),
            jax.ShapeDtypeStruct((1, rows), f32),
            jax.ShapeDtypeStruct((1, cols), f32),
        )
        new_w, row_moment, col_moment = pl.pallas_call(
            kernel,
            out_shape=shapes,
            in_specs=[hbm] * 5,
            out_specs=(vmem,) * 3,
            scratch_shapes=[
                pltpu.VMEM((2 * NX, rows, cols), jnp.bfloat16),
                pltpu.VMEM((NX, rows, cols), f32),
                pltpu.VMEM((NX, rows, cols), f32),
                pltpu.VMEM((CHUNKS, 2, rc, cols // 2), f32),
                pltpu.VMEM((CHUNKS, 2, rc, cols // 2), f32),
                pltpu.VMEM((CHUNKS, 2, rc, cols), f32),
                pltpu.VMEM((CHUNKS, 2, rc, cols), f32),
                pltpu.VMEM((rows, cols), f32),
                pltpu.VMEM((rows, cols), jnp.bfloat16),
                pltpu.VMEM((1, rows), f32),
                pltpu.VMEM((1, cols), f32),
                pltpu.VMEM((1, 1), f32),
                pltpu.VMEM((NX * NCORE * NZLO, 1, LANES), f32),
                pltpu.VMEM((NY * NZHI, 8, LANES), f32),
                pltpu.VMEM((NX * NCORE * NZLO, 1, LANES), f32),
                dma((2 * NX,)), dma((4,)),
                dma((CHUNKS + 3,)), dma((CHUNKS + 3,)),
                dma((CHUNKS, 2)), dma((CHUNKS, 2)),
                dma((CHUNKS, 2)), dma((CHUNKS, 2)),
                dma((3,)), dma((3,)),
                pltpu.SemaphoreType.REGULAR((4,)),
            ],
            compiler_params=pltpu.CompilerParams(collective_id=0, has_side_effects=True, vmem_limit_bytes=63 << 20),
        )(grad_parts.reshape(rows, width), weights.reshape(rows, cols), row_old, col_old.reshape(1, cols), step_rates.reshape(1, 1))
        return new_w.reshape(weights.shape), row_moment, col_moment.reshape(col_old.shape)

    in_specs = (
        P("dp", None, "row", "col", None),
        P(None, "row", "col", "dp"),
        P(None, "row"),
        P(None, "col", "dp"),
        P(),
    )
    out_specs = (P(None, "row", "col", "dp"), P(None, "row"), P(None, "col", "dp"))
    return jax.shard_map(per_device, mesh=mesh, in_specs=in_specs, out_specs=out_specs, check_vma=False)
```

```python
import functools

import jax
import jax.numpy as jnp
from jax import lax
from jax.experimental import pallas as pl
from jax.experimental.pallas import tpu as pltpu
from jax.sharding import PartitionSpec as P

D = 4096
QKV = 12288
EPS = 1e-30
MESH = pl.DeviceIdType.MESH
CHUNKS = 4
LANES = 128
NX, NCORE, NY, NZHI, NZLO = 4, 2, 8, 4, 3
NZ = NZHI * NZLO


def kernel(g_hbm, ro_hbm, co_hbm, sr_hbm, gf, step_ref, orow_ref, ocol_ref,
           gb, snd, prt, fs, fr, js, jr, ds, dr, ro, co, sr, rowbuf, colbuf, totbuf,
           load_sem, misc_sem, core_send, core_recv, f_send, f_recv, j_send, j_recv, d_send, d_recv, ar_send, ar_recv, met):
    rows, cols = gf.shape
    half = cols // 2
    groups = cols // LANES
    rc = rows // CHUNKS
    n_flat = NX * NCORE * NZLO
    n_row = NY * NZHI

    dp = lax.axis_index("dp")
    row = lax.axis_index("row")
    col = lax.axis_index("col")
    x, core = lax.div(dp, NCORE), lax.rem(dp, NCORE)
    y, zhi = lax.div(row, NZHI), lax.rem(row, NZHI)
    z = zhi * NZLO + col
    me = dp * NZLO + col

    def at(dx=0, dc=0, dy=0, dz=0):
        zz = lax.rem(z + dz + NZ, NZ)
        return {
            "dp": lax.rem(x + dx + NX, NX) * NCORE + lax.rem(core + dc, NCORE),
            "row": lax.rem(y + dy + NY, NY) * NZHI + lax.div(zz, NZLO),
            "col": lax.rem(zz, NZLO),
        }

    def flat_at(dx, dc, k):
        return {"dp": lax.rem(x + dx, NX) * NCORE + lax.rem(core + dc, NCORE), "row": row, "col": lax.rem(col + k, NZLO)}

    def row_at(dy, dz):
        return {"dp": dp, "row": lax.rem(y + dy, NY) * NZHI + lax.rem(zhi + dz, NZHI), "col": col}

    flat_peers = [flat_at(dx, dc, k) for dx in (2, 1, 3, 0) for k in (1, 2, 0) for dc in (1, 0) if dx or dc or k]
    row_peers = [row_at(dy, dz) for dy, dz in sorted(
        ((dy, dz) for dy in range(NY) for dz in range(NZHI) if dy or dz),
        key=lambda p: -(min(p[0], NY - p[0]) + 3 * min(p[1], NZHI - p[1])))]

    near = [at(dc=1), at(dx=1), at(dx=-1), at(dy=1), at(dy=-1), at(dz=1), at(dz=-1)]
    steps = [
        near,
        [at(dc=1), at(dx=2), at(dy=2), at(dy=-2), at(dz=2), at(dz=-2)],
        [at(dc=1), at(dz=3), at(dz=-3)],
        [at(dz=3), at(dz=-3)],
    ]

    barrier = pltpu.get_barrier_semaphore()
    for d in near:
        pl.semaphore_signal(barrier, inc=1, device_id=d, device_id_type=MESH)

    def tell(s):
        for d in steps[s]:
            pl.semaphore_signal(met.at[s], inc=1, device_id=d, device_id_type=MESH)

    def hear(s):
        pl.semaphore_wait(met.at[s], len(steps[s]))

    def load(rel, who):
        j = lax.rem(x + rel, NX) * NCORE + (core if who == 0 else 1 - core)
        i = 2 * rel + who
        return pltpu.make_async_copy(
            g_hbm.at[:, pl.ds(pl.multiple_of(j * cols, cols), cols)], gb.at[i], load_sem.at[i])

    order = (2, 1, 3, 0)
    for rel in order:
        for who in (1, 0):
            load(rel, who).start()
    misc = [pltpu.make_async_copy(a, b, misc_sem.at[i])
            for i, (a, b) in enumerate(((ro_hbm, ro), (co_hbm, co), (sr_hbm, sr)))]
    for m in misc:
        m.start()

    def part(rel, who, rs, side=None):
        cs = slice(None) if side is None else halves[side]
        return gb[2 * rel + who, rs, cs].astype(jnp.float32)

    def chunk(k):
        return pl.ds(k * rc, rc)

    def core_copy(i):
        if i < CHUNKS:
            src, dst = snd.at[2, chunk(i)], prt.at[2, chunk(i)]
        else:
            src, dst = snd.at[order[i - CHUNKS + 1]], prt.at[order[i - CHUNKS + 1]]
        return pltpu.make_async_remote_copy(
            src_ref=src, dst_ref=dst, send_sem=core_send.at[i], recv_sem=core_recv.at[i],
            device_id=at(dc=1), device_id_type=MESH)

    n_core = CHUNKS + 3

    halves = (pl.ds(0, half), pl.ds(half, half))

    def hop(buf, out, idx, side, send_sem, recv_sem):
        return pltpu.make_async_remote_copy(
            src_ref=buf.at[idx], dst_ref=out.at[idx], send_sem=send_sem.at[idx], recv_sem=recv_sem.at[idx],
            device_id=at(dx=1 if side == 0 else -1), device_id_type=MESH)

    whole = pl.ds(0, rows)
    for n, rel in enumerate(order):
        load(rel, 1).wait()
        snd[rel] = part(rel, 1, whole)
        if n == 0:
            pl.semaphore_wait(barrier, len(near))
            for i in range(CHUNKS):
                core_copy(i).start()
        else:
            core_copy(CHUNKS + n - 1).start()
    tell(0)

    load(2, 0).wait()
    for k in range(CHUNKS):
        core_copy(k).wait_recv()
        far = part(2, 0, chunk(k)) + prt[2, chunk(k), :]
        for side in range(2):
            fs[k, side] = far[:, side * half:(side + 1) * half]
            hop(fs, fr, (k, side), side, f_send, f_recv).start()
    hear(0)
    tell(1)
    for side, rel in ((0, 1), (1, 3)):
        load(rel, 0).wait()
        core_copy(CHUNKS + side).wait_recv()
        js[side] = part(rel, 0, whole, 1 - side) + prt[rel, :, halves[1 - side]]
        hop(js, jr, (side,), side, j_send, j_recv).start()
    for k in range(CHUNKS):
        for side, rel in ((0, 1), (1, 3)):
            near_sum = part(rel, 0, chunk(k), side) + prt[rel, chunk(k), halves[side]]
            hop(fs, fr, (k, side), side, f_send, f_recv).wait_recv()
            ds[k, side] = near_sum + fr[k, side]
            hop(ds, dr, (k, side), side, d_send, d_recv).start()
    hear(1)
    tell(2)
    load(0, 0).wait()
    core_copy(CHUNKS + 2).wait_recv()
    for m in misc:
        m.wait()
    for side in range(2):
        hop(js, jr, (side,), side, j_send, j_recv).wait_recv()
    for side in range(2):
        gf[:, halves[side]] = part(0, 0, whole, side) + prt[0, :, halves[side]] + jr[1 - side]
    for k in range(CHUNKS):
        for side in range(2):
            hop(ds, dr, (k, side), side, d_send, d_recv).wait_recv()
            gf[chunk(k), halves[side]] = gf[chunk(k), halves[side]] + dr[k, side]

    def exchange(buf, slot, peers, i):
        for d in peers:
            pltpu.make_async_remote_copy(
                src_ref=buf.at[slot], dst_ref=buf.at[slot], send_sem=ar_send.at[i], recv_sem=ar_recv.at[i],
                device_id=d, device_id_type=MESH).start()

    def all_of(buf, n, i):
        return pltpu.make_async_remote_copy(
            src_ref=buf.at[pl.ds(0, n)], dst_ref=buf.at[pl.ds(0, n)], send_sem=ar_send.at[i], recv_sem=ar_recv.at[i],
            device_id=at(dc=1), device_id_type=MESH)

    def lane(q):
        return slice(q * LANES, (q + 1) * LANES)

    acc = jnp.zeros((rows, LANES), jnp.float32)
    for q in range(groups):
        v = gf[:, lane(q)]
        acc = acc + (v * v + EPS)
    rowbuf[me] = jnp.sum(acc.T, axis=0, keepdims=True)
    hear(2)
    exchange(rowbuf, me, flat_peers, 0)
    tell(3)
    for q in range(groups):
        v = gf[:, lane(q)]
        colbuf[row, q:q + 1, :] = jnp.sum(v * v + EPS, axis=0, keepdims=True)
    all_of(rowbuf, n_flat - 1, 0).wait_recv()
    row_sum = jnp.sum(rowbuf[...], axis=0)
    row_moment = 0.8 * ro[...] + 0.2 * row_sum / QKV
    orow_ref[...] = row_moment
    scale = jnp.broadcast_to(lax.rsqrt(row_moment), (LANES, rows)).T

    for q in range(groups):
        h = gf[:, lane(q)] * scale
        gf[:, lane(q)] = h
        colbuf[row, groups + q:groups + q + 1, :] = jnp.sum(h * h, axis=0, keepdims=True)
    hear(3)
    exchange(colbuf, row, row_peers, 1)
    all_of(colbuf, n_row - 1, 1).wait_recv()
    both = jnp.sum(colbuf[...], axis=0)
    total_part = jnp.zeros((1, LANES), jnp.float32)
    for q in range(groups):
        col_moment = 0.8 * co[:, lane(q)] + 0.2 * both[q:q + 1] / D
        ocol_ref[:, lane(q)] = col_moment
        total_part = total_part + both[groups + q:groups + q + 1] / col_moment
    totbuf[me] = total_part
    exchange(totbuf, me, flat_peers, 2)
    for q in range(groups):
        gf[:, lane(q)] = gf[:, lane(q)] * lax.rsqrt(ocol_ref[:, lane(q)])
    all_of(totbuf, n_flat - 1, 2).wait_recv()
    total = jnp.sum(jnp.sum(totbuf[...], axis=0), axis=1, keepdims=True)
    clip = 1.0 / jnp.maximum(1.0, jnp.sqrt(total / (D * QKV)) / 0.2)
    step_ref[...] = jnp.broadcast_to(sr[...] * clip, step_ref.shape)

    for i in range(n_core):
        core_copy(i).wait_send()
    for k in range(CHUNKS):
        for side in range(2):
            hop(fs, fr, (k, side), side, f_send, f_recv).wait_send()
            hop(ds, dr, (k, side), side, d_send, d_recv).wait_send()
    for side in range(2):
        hop(js, jr, (side,), side, j_send, j_recv).wait_send()
    all_of(rowbuf, n_flat - 1, 0).wait_send()
    all_of(colbuf, n_row - 1, 1).wait_send()
    all_of(totbuf, n_flat - 1, 2).wait_send()


def apply(u_ref, step_ref, row_ref, col_ref, w_ref, ow_hbm, orow_hbm, ocol_hbm, nw, sem):
    def out(i, a, b):
        return pltpu.make_async_copy(a, b, sem.at[i])

    small = [out(0, row_ref, orow_hbm), out(1, col_ref, ocol_hbm)]
    for c in small:
        c.start()
    nw[...] = (w_ref[...].astype(jnp.float32) - step_ref[0:1, 0:1] * u_ref[...]).astype(jnp.bfloat16)
    big = out(2, nw, ow_hbm)
    big.start()
    for c in small + [big]:
        c.wait()


def solution(mesh):
    def per_device(grad_parts, weights, row_old, col_old, step_rates):
        rows, width = grad_parts.shape[2], grad_parts.shape[4]
        cols = weights.shape[3]
        rc = rows // CHUNKS
        f32 = jnp.float32
        keep = functools.partial(pltpu.with_memory_space_constraint, memory_space=pltpu.HBM)
        vmem = pl.BlockSpec(memory_space=pltpu.VMEM)
        hbm = pl.BlockSpec(memory_space=pltpu.HBM)
        dma = pltpu.SemaphoreType.DMA
        shapes = (
            jax.ShapeDtypeStruct((1, rows), f32),
            jax.ShapeDtypeStruct((1, cols), f32),
        )
        update, step, row_moment, col_moment = pl.pallas_call(
            kernel,
            out_shape=(jax.ShapeDtypeStruct((rows, cols), f32), jax.ShapeDtypeStruct((1, LANES), f32)) + shapes,
            in_specs=[hbm] * 4,
            out_specs=(vmem,) * 4,
            scratch_shapes=[
                pltpu.VMEM((2 * NX, rows, cols), jnp.bfloat16),
                pltpu.VMEM((NX, rows, cols), f32),
                pltpu.VMEM((NX, rows, cols), f32),
                pltpu.VMEM((CHUNKS, 2, rc, cols // 2), f32),
                pltpu.VMEM((CHUNKS, 2, rc, cols // 2), f32),
                pltpu.VMEM((2, rows, cols // 2), f32),
                pltpu.VMEM((2, rows, cols // 2), f32),
                pltpu.VMEM((CHUNKS, 2, rc, cols // 2), f32),
                pltpu.VMEM((CHUNKS, 2, rc, cols // 2), f32),
                pltpu.VMEM((1, rows), f32),
                pltpu.VMEM((1, cols), f32),
                pltpu.VMEM((1, 1), f32),
                pltpu.VMEM((NX * NCORE * NZLO, 1, LANES), f32),
                pltpu.VMEM((NY * NZHI, 8, LANES), f32),
                pltpu.VMEM((NX * NCORE * NZLO, 1, LANES), f32),
                dma((2 * NX,)), dma((3,)),
                dma((CHUNKS + 3,)), dma((CHUNKS + 3,)),
                dma((CHUNKS, 2)), dma((CHUNKS, 2)),
                dma((2,)), dma((2,)),
                dma((CHUNKS, 2)), dma((CHUNKS, 2)),
                dma((3,)), dma((3,)),
                pltpu.SemaphoreType.REGULAR((4,)),
            ],
            compiler_params=pltpu.CompilerParams(collective_id=0, has_side_effects=True, vmem_limit_bytes=32 << 20),
        )(keep(grad_parts.reshape(rows, width)), keep(row_old), keep(col_old.reshape(1, cols)), step_rates.reshape(1, 1))
        new_w, row_moment, col_moment = pl.pallas_call(
            apply,
            out_shape=(jax.ShapeDtypeStruct((rows, cols), jnp.bfloat16),) + shapes,
            in_specs=[vmem] * 5,
            out_specs=(pl.BlockSpec(memory_space=pl.ANY),) * 3,
            scratch_shapes=[pltpu.VMEM((rows, cols), jnp.bfloat16), dma((3,))],
            compiler_params=pltpu.CompilerParams(vmem_limit_bytes=4 << 20),
        )(update, step, row_moment, col_moment, weights.reshape(rows, cols))
        return new_w.reshape(weights.shape), row_moment, col_moment.reshape(col_old.shape)

    in_specs = (
        P("dp", None, "row", "col", None),
        P(None, "row", "col", "dp"),
        P(None, "row"),
        P(None, "col", "dp"),
        P(),
    )
    out_specs = (P(None, "row", "col", "dp"), P(None, "row"), P(None, "col", "dp"))
    return jax.shard_map(per_device, mesh=mesh, in_specs=in_specs, out_specs=out_specs, check_vma=False)
```

```python
import functools

import jax
import jax.numpy as jnp
from jax import lax
from jax.experimental import pallas as pl
from jax.experimental.pallas import tpu as pltpu
from jax.sharding import PartitionSpec as P

D = 4096
QKV = 12288
EPS = 1e-30
MESH = pl.DeviceIdType.MESH
CHUNKS = 4
LANES = 128
NX, NCORE, NY, NZHI, NZLO = 4, 2, 8, 4, 3
NZ = NZHI * NZLO


def kernel(g_hbm, ro_hbm, co_hbm, sr_hbm, gf, step_ref, orow_ref, ocol_ref,
           gb, snd, prt, fs, fr, js, jr, ds, dr, ro, co, sr, rowbuf, colbuf, totbuf,
           load_sem, misc_sem, core_send, core_recv, f_send, f_recv, j_send, j_recv, d_send, d_recv, ar_send, ar_recv, met):
    rows, cols = gf.shape
    half = cols // 2
    groups = cols // LANES
    rc = rows // CHUNKS
    n_flat = NX * NCORE * NZLO
    n_row = NY * NZHI

    dp = lax.axis_index("dp")
    row = lax.axis_index("row")
    col = lax.axis_index("col")
    x, core = lax.div(dp, NCORE), lax.rem(dp, NCORE)
    y, zhi = lax.div(row, NZHI), lax.rem(row, NZHI)
    z = zhi * NZLO + col
    me = dp * NZLO + col

    def at(dx=0, dc=0, dy=0, dz=0):
        zz = lax.rem(z + dz + NZ, NZ)
        return {
            "dp": lax.rem(x + dx + NX, NX) * NCORE + lax.rem(core + dc, NCORE),
            "row": lax.rem(y + dy + NY, NY) * NZHI + lax.div(zz, NZLO),
            "col": lax.rem(zz, NZLO),
        }

    def flat_at(dx, dc, k):
        return {"dp": lax.rem(x + dx, NX) * NCORE + lax.rem(core + dc, NCORE), "row": row, "col": lax.rem(col + k, NZLO)}

    def row_at(dy, dz):
        return {"dp": dp, "row": lax.rem(y + dy, NY) * NZHI + lax.rem(zhi + dz, NZHI), "col": col}

    flat_peers = [flat_at(dx, dc, k) for dx in (2, 1, 3, 0) for k in (1, 2, 0) for dc in (1, 0) if dx or dc or k]
    row_peers = [row_at(dy, dz) for dy, dz in sorted(
        ((dy, dz) for dy in range(NY) for dz in range(NZHI) if dy or dz),
        key=lambda p: -(min(p[0], NY - p[0]) + 3 * min(p[1], NZHI - p[1])))]

    near = [at(dc=1), at(dx=1), at(dx=-1), at(dy=1), at(dy=-1), at(dz=1), at(dz=-1)]
    steps = [
        near,
        [at(dc=1), at(dx=2), at(dy=2), at(dy=-2), at(dz=2), at(dz=-2)],
        [at(dc=1), at(dz=3), at(dz=-3)],
        [at(dz=3), at(dz=-3)],
    ]

    barrier = pltpu.get_barrier_semaphore()
    for d in (at(dc=1), at(dx=1), at(dx=-1)):
        pl.semaphore_signal(barrier, inc=1, device_id=d, device_id_type=MESH)
    greets = 3
    answers = 0
    replies = []
    for place, size, up, down in ((z, NZ, at(dz=1), at(dz=-1)), (y, NY, at(dy=1), at(dy=-1))):
        first, last = place == 0, place == size - 1
        greets = greets + jnp.where(first, 0, 1) + jnp.where(last, 1, 0)
        answers = answers + jnp.where(last, 0, 1) + jnp.where(first, 1, 0)
        for ok, d in ((jnp.logical_not(last), up), (first, down)):
            @pl.when(ok)
            def _(d=d):
                pl.semaphore_signal(barrier, inc=1, device_id=d, device_id_type=MESH)
        replies += [(jnp.logical_not(first), down), (last, up)]

    def reply():
        for ok, d in replies:
            @pl.when(ok)
            def _(d=d):
                pl.semaphore_signal(met.at[4], inc=1, device_id=d, device_id_type=MESH)

    def tell(s):
        for d in steps[s]:
            pl.semaphore_signal(met.at[s], inc=1, device_id=d, device_id_type=MESH)

    def hear(s):
        pl.semaphore_wait(met.at[s], len(steps[s]))

    def load(rel, who):
        j = lax.rem(x + rel, NX) * NCORE + (core if who == 0 else 1 - core)
        i = 2 * rel + who
        return pltpu.make_async_copy(
            g_hbm.at[:, pl.ds(pl.multiple_of(j * cols, cols), cols)], gb.at[i], load_sem.at[i])

    order = (2, 1, 3, 0)
    for rel in order:
        for who in (1, 0):
            load(rel, who).start()
    misc = [pltpu.make_async_copy(a, b, misc_sem.at[i])
            for i, (a, b) in enumerate(((ro_hbm, ro), (co_hbm, co), (sr_hbm, sr)))]
    for m in misc:
        m.start()

    def part(rel, who, rs, side=None):
        cs = slice(None) if side is None else halves[side]
        return gb[2 * rel + who, rs, cs].astype(jnp.float32)

    def chunk(k):
        return pl.ds(k * rc, rc)

    def core_copy(i):
        if i < CHUNKS:
            src, dst = snd.at[2, chunk(i)], prt.at[2, chunk(i)]
        else:
            src, dst = snd.at[order[i - CHUNKS + 1]], prt.at[order[i - CHUNKS + 1]]
        return pltpu.make_async_remote_copy(
            src_ref=src, dst_ref=dst, send_sem=core_send.at[i], recv_sem=core_recv.at[i],
            device_id=at(dc=1), device_id_type=MESH)

    n_core = CHUNKS + 3

    halves = (pl.ds(0, half), pl.ds(half, half))

    def hop(buf, out, idx, side, send_sem, recv_sem):
        return pltpu.make_async_remote_copy(
            src_ref=buf.at[idx], dst_ref=out.at[idx], send_sem=send_sem.at[idx], recv_sem=recv_sem.at[idx],
            device_id=at(dx=1 if side == 0 else -1), device_id_type=MESH)

    whole = pl.ds(0, rows)
    for n, rel in enumerate(order):
        load(rel, 1).wait()
        snd[rel] = part(rel, 1, whole)
        if n == 0:
            pl.semaphore_wait(barrier, greets)
            reply()
            for i in range(CHUNKS):
                core_copy(i).start()
        else:
            core_copy(CHUNKS + n - 1).start()

    load(2, 0).wait()
    for k in range(CHUNKS):
        core_copy(k).wait_recv()
        far = part(2, 0, chunk(k)) + prt[2, chunk(k), :]
        for side in range(2):
            fs[k, side] = far[:, side * half:(side + 1) * half]
            hop(fs, fr, (k, side), side, f_send, f_recv).start()
    @pl.when(answers > 0)
    def _():
        pl.semaphore_wait(met.at[4], answers)

    tell(0)
    for side, rel in ((0, 1), (1, 3)):
        load(rel, 0).wait()
        core_copy(CHUNKS + side).wait_recv()
        js[side] = part(rel, 0, whole, 1 - side) + prt[rel, :, halves[1 - side]]
        hop(js, jr, (side,), side, j_send, j_recv).start()
    hear(0)
    tell(1)
    for k in range(CHUNKS):
        for side, rel in ((0, 1), (1, 3)):
            near_sum = part(rel, 0, chunk(k), side) + prt[rel, chunk(k), halves[side]]
            hop(fs, fr, (k, side), side, f_send, f_recv).wait_recv()
            ds[k, side] = near_sum + fr[k, side]
            hop(ds, dr, (k, side), side, d_send, d_recv).start()
    hear(1)
    tell(2)
    load(0, 0).wait()
    core_copy(CHUNKS + 2).wait_recv()
    for m in misc:
        m.wait()
    for side in range(2):
        hop(js, jr, (side,), side, j_send, j_recv).wait_recv()
    for side in range(2):
        gf[:, halves[side]] = part(0, 0, whole, side) + prt[0, :, halves[side]] + jr[1 - side]
    for k in range(CHUNKS):
        for side in range(2):
            hop(ds, dr, (k, side), side, d_send, d_recv).wait_recv()
            gf[chunk(k), halves[side]] = gf[chunk(k), halves[side]] + dr[k, side]

    def exchange(buf, slot, peers, i):
        for d in peers:
            pltpu.make_async_remote_copy(
                src_ref=buf.at[slot], dst_ref=buf.at[slot], send_sem=ar_send.at[i], recv_sem=ar_recv.at[i],
                device_id=d, device_id_type=MESH).start()

    def all_of(buf, n, i):
        return pltpu.make_async_remote_copy(
            src_ref=buf.at[pl.ds(0, n)], dst_ref=buf.at[pl.ds(0, n)], send_sem=ar_send.at[i], recv_sem=ar_recv.at[i],
            device_id=at(dc=1), device_id_type=MESH)

    def lane(q):
        return slice(q * LANES, (q + 1) * LANES)

    acc = jnp.zeros((rows, LANES), jnp.float32)
    for q in range(groups):
        v = gf[:, lane(q)]
        acc = acc + (v * v + EPS)
    rowbuf[me] = jnp.sum(acc.T, axis=0, keepdims=True)
    hear(2)
    exchange(rowbuf, me, flat_peers, 0)
    tell(3)
    for q in range(groups):
        v = gf[:, lane(q)]
        colbuf[row, q:q + 1, :] = jnp.sum(v * v + EPS, axis=0, keepdims=True)
    all_of(rowbuf, n_flat - 1, 0).wait_recv()
    row_sum = jnp.sum(rowbuf[...], axis=0)
    row_moment = 0.8 * ro[...] + 0.2 * row_sum / QKV
    orow_ref[...] = row_moment
    scale = jnp.broadcast_to(lax.rsqrt(row_moment), (LANES, rows)).T

    for q in range(groups):
        h = gf[:, lane(q)] * scale
        gf[:, lane(q)] = h
        colbuf[row, groups + q:groups + q + 1, :] = jnp.sum(h * h, axis=0, keepdims=True)
    hear(3)
    exchange(colbuf, row, row_peers, 1)
    all_of(colbuf, n_row - 1, 1).wait_recv()
    both = jnp.sum(colbuf[...], axis=0)
    total_part = jnp.zeros((1, LANES), jnp.float32)
    for q in range(groups):
        col_moment = 0.8 * co[:, lane(q)] + 0.2 * both[q:q + 1] / D
        ocol_ref[:, lane(q)] = col_moment
        total_part = total_part + both[groups + q:groups + q + 1] / col_moment
    totbuf[me] = total_part
    exchange(totbuf, me, flat_peers, 2)
    for q in range(groups):
        gf[:, lane(q)] = gf[:, lane(q)] * lax.rsqrt(ocol_ref[:, lane(q)])
    for i in range(n_core):
        core_copy(i).wait_send()
    for k in range(CHUNKS):
        for side in range(2):
            hop(fs, fr, (k, side), side, f_send, f_recv).wait_send()
            hop(ds, dr, (k, side), side, d_send, d_recv).wait_send()
    for side in range(2):
        hop(js, jr, (side,), side, j_send, j_recv).wait_send()
    all_of(rowbuf, n_flat - 1, 0).wait_send()
    all_of(colbuf, n_row - 1, 1).wait_send()
    all_of(totbuf, n_flat - 1, 2).wait_recv()
    total = jnp.sum(jnp.sum(totbuf[...], axis=0), axis=1, keepdims=True)
    clip = 1.0 / jnp.maximum(1.0, jnp.sqrt(total / (D * QKV)) / 0.2)
    step_ref[...] = jnp.broadcast_to(sr[...] * clip, step_ref.shape)
    all_of(totbuf, n_flat - 1, 2).wait_send()


def apply(u_ref, step_ref, row_ref, col_ref, w_ref, ow_hbm, orow_hbm, ocol_hbm, nw, sem):
    def out(i, a, b):
        return pltpu.make_async_copy(a, b, sem.at[i])

    small = [out(0, row_ref, orow_hbm), out(1, col_ref, ocol_hbm)]
    for c in small:
        c.start()
    nw[...] = (w_ref[...].astype(jnp.float32) - step_ref[0:1, 0:1] * u_ref[...]).astype(jnp.bfloat16)
    big = out(2, nw, ow_hbm)
    big.start()
    for c in small + [big]:
        c.wait()


def solution(mesh):
    def per_device(grad_parts, weights, row_old, col_old, step_rates):
        rows, width = grad_parts.shape[2], grad_parts.shape[4]
        cols = weights.shape[3]
        rc = rows // CHUNKS
        f32 = jnp.float32
        keep = functools.partial(pltpu.with_memory_space_constraint, memory_space=pltpu.HBM)
        vmem = pl.BlockSpec(memory_space=pltpu.VMEM)
        hbm = pl.BlockSpec(memory_space=pltpu.HBM)
        dma = pltpu.SemaphoreType.DMA
        shapes = (
            jax.ShapeDtypeStruct((1, rows), f32),
            jax.ShapeDtypeStruct((1, cols), f32),
        )
        update, step, row_moment, col_moment = pl.pallas_call(
            kernel,
            out_shape=(jax.ShapeDtypeStruct((rows, cols), f32), jax.ShapeDtypeStruct((1, LANES), f32)) + shapes,
            in_specs=[hbm] * 4,
            out_specs=(vmem,) * 4,
            scratch_shapes=[
                pltpu.VMEM((2 * NX, rows, cols), jnp.bfloat16),
                pltpu.VMEM((NX, rows, cols), f32),
                pltpu.VMEM((NX, rows, cols), f32),
                pltpu.VMEM((CHUNKS, 2, rc, cols // 2), f32),
                pltpu.VMEM((CHUNKS, 2, rc, cols // 2), f32),
                pltpu.VMEM((2, rows, cols // 2), f32),
                pltpu.VMEM((2, rows, cols // 2), f32),
                pltpu.VMEM((CHUNKS, 2, rc, cols // 2), f32),
                pltpu.VMEM((CHUNKS, 2, rc, cols // 2), f32),
                pltpu.VMEM((1, rows), f32),
                pltpu.VMEM((1, cols), f32),
                pltpu.VMEM((1, 1), f32),
                pltpu.VMEM((NX * NCORE * NZLO, 1, LANES), f32),
                pltpu.VMEM((NY * NZHI, 8, LANES), f32),
                pltpu.VMEM((NX * NCORE * NZLO, 1, LANES), f32),
                dma((2 * NX,)), dma((3,)),
                dma((CHUNKS + 3,)), dma((CHUNKS + 3,)),
                dma((CHUNKS, 2)), dma((CHUNKS, 2)),
                dma((2,)), dma((2,)),
                dma((CHUNKS, 2)), dma((CHUNKS, 2)),
                dma((3,)), dma((3,)),
                pltpu.SemaphoreType.REGULAR((5,)),
            ],
            compiler_params=pltpu.CompilerParams(collective_id=0, has_side_effects=True, vmem_limit_bytes=32 << 20),
        )(keep(grad_parts.reshape(rows, width)), keep(row_old), keep(col_old.reshape(1, cols)), step_rates.reshape(1, 1))
        new_w, row_moment, col_moment = pl.pallas_call(
            apply,
            out_shape=(jax.ShapeDtypeStruct((rows, cols), jnp.bfloat16),) + shapes,
            in_specs=[vmem] * 5,
            out_specs=(pl.BlockSpec(memory_space=pl.ANY),) * 3,
            scratch_shapes=[pltpu.VMEM((rows, cols), jnp.bfloat16), dma((3,))],
            compiler_params=pltpu.CompilerParams(vmem_limit_bytes=4 << 20),
        )(update, step, row_moment, col_moment, weights.reshape(rows, cols))
        return new_w.reshape(weights.shape), row_moment, col_moment.reshape(col_old.shape)

    in_specs = (
        P("dp", None, "row", "col", None),
        P(None, "row", "col", "dp"),
        P(None, "row"),
        P(None, "col", "dp"),
        P(),
    )
    out_specs = (P(None, "row", "col", "dp"), P(None, "row"), P(None, "col", "dp"))
    return jax.shard_map(per_device, mesh=mesh, in_specs=in_specs, out_specs=out_specs, check_vma=False)
```
